32 devices in a mesh: grp: 2 (over y), kz: 4 (over z), coil: 2 (over x), kx: 2 (over core).
Axes of the slice: x: 2, y: 2, z: 4, core: 2. Of those that a mesh axis runs over, the one named last changes fastest.
Arguments:
- measured: float32 [2, 64, 32, 32, 32], P(None, ('grp', 'coil'), 'kx', 'kz'), parts along dimension 1, may hold values from -6 to 6
- mask: int32 [64, 32, 32], P(('grp', 'kx'), 'kz'), parts along dimension 0, may hold values 0 or 1
- kernel: float32 [27, 2, 32, 64], P(None, None, 'coil'), may hold values from -0.109375 to 0.109375
Outputs:
- restored: float32 [2, 64, 32, 32, 32], P(None, ('grp', 'coil'), 'kx', 'kz'), parts along dimension 1
The draws below stay inside these ranges and needn't reach their ends.
There are 2 independent parts, one for each index of `grp`. The reference program is written for one: setup_inputs(seed, part) draws one part's arguments, and reference() takes and returns one part's arrays. A program takes and returns all parts, laid end to end along the dimension named above; an argument that names none is the same for every part. Nothing has to cross between parts.
All inputs are finite; a program needn't handle non-finite values. No bound on the sum of `mask` on one device may be relied on, other than what follows from the above.
Results may differ from the reference program's by a relative error of at most 0.0001.
Values sent between devices are 32-bit elements; how exact they have to be, the bound alone decides.
A program may use at most 128 MiB of HBM per device.

```python
import jax
import jax.numpy as jnp
from jax import lax

COILS = 32
KX = 32
KY = 32
ITERS = 2
TAPS = 27
KZ = 32


def touch_ends(drawn, rng, low, largest):
    longest = drawn.shape.index(max(drawn.shape))
    spots = []
    for shift in (0, 1):
        where = [jax.random.randint(jax.random.fold_in(rng, axis), (), 0, length) for axis, length in enumerate(drawn.shape)]
        where[longest] = (where[longest] + shift) % drawn.shape[longest]
        spots.append(tuple(where))
    return drawn.at[spots[0]].set(low).at[spots[1]].set(largest)


def steps_of(own_key, shape, shards, low, high):
    loudness = 1.0
    for position, parts in shards:
        heights = jax.random.uniform(jax.random.fold_in(jax.random.fold_in(own_key, 6), position), (parts,), jnp.float32, low / len(shards), high / len(shards))
        loudness = loudness * jnp.repeat(jnp.exp(heights), shape[position] // parts).reshape((-1,) + (1,) * (len(shape) - 1 - position))
    return loudness


def bell_draw(key, extent, width, bound, shards=(), kind=jnp.bfloat16):
    entries = jax.random.normal(key, extent, jnp.float32) * width
    if len(shards) > 0:
        entries = steps_of(key, extent, shards, -0.22, 0.18) * entries
    return jnp.clip(entries, min=-bound, max=bound).astype(kind)


def setup_inputs(seed: int = 0, part: int = 0) -> dict:
    key_list = jax.random.split(jax.random.key(seed), 4)
    part_keys = jax.random.split(jax.random.fold_in(key_list[3], part), 4)
    measured = bell_draw(part_keys[0], (2, COILS, KX, KZ, KY), 1.0, 6.0, ((1, 2), (2, 2), (3, 4)), jnp.float32)
    mask = touch_ends((jax.random.randint(part_keys[1], (KX, KZ, KY), 0, 2) < 1).astype(jnp.int32), jax.random.fold_in(part_keys[1], 1), 0, 1)
    kernel = bell_draw(key_list[2], (TAPS, 2, COILS, 2 * COILS), (108 * COILS) ** -0.5, 0.109375, ((2, 2),), jnp.float32)
    return {"measured": measured, "mask": mask, "kernel": kernel}


def reference(measured, mask, kernel):
    sampled = (mask == 1)[None, None]
    state = jnp.where(sampled, measured, jnp.zeros_like(measured))
    real_k = kernel[:, 0]
    imag_k = kernel[:, 1]
    weights = jnp.concatenate([jnp.concatenate([real_k, -imag_k], 2), jnp.concatenate([imag_k, real_k], 2)], 1)
    sign = jnp.array([1.0, -1.0], jnp.float32).reshape(2, 1, 1, 1, 1)
    for step in range(ITERS):
        virtual = jnp.flip(state, (2, 3, 4)) * sign
        stacked = jnp.concatenate([state, virtual], 1)
        padded = jnp.pad(stacked, ((0, 0), (0, 0), (1, 1), (1, 1), (1, 1)))
        result = jnp.zeros(state.shape, jnp.float32)
        for first in range(3):
            for second in range(3):
                for third in range(3):
                    window = padded[:, :, first:first + KX, third:third + KZ, second:second + KY]
                    window = window.reshape(4 * COILS, -1)
                    term = jnp.dot(weights[9 * first + 3 * second + third], window, precision=lax.Precision.HIGHEST)
                    result = result + term.reshape(state.shape)
        state = jnp.where(sampled, measured, result)
    return state
```

```python
import functools

import jax
import jax.numpy as jnp
from jax import lax
from jax.experimental import pallas as pl
from jax.experimental.pallas import tpu as pltpu
from jax.sharding import PartitionSpec as P

ITERS = 2
LANES = 128
MESH = pl.DeviceIdType.MESH


def build_weights(kernel, shards):
    coils = kernel.shape[2]
    k = kernel.reshape(3, 3, 3, 2, coils, 2, shards, coils)
    re, im = k[:, :, :, 0], k[:, :, :, 1]
    pr, pi = re[:, :, :, :, 0], im[:, :, :, :, 0]
    vr, vi = (jnp.flip(x[:, :, :, :, 1], (0, 1, 2)) for x in (re, im))

    def block(q):
        return jnp.stack([jnp.stack(row, 0) for row in q], 0)

    w = jnp.stack([block(((pr, -pi), (pi, pr))), block(((vr, vi), (vi, -vr)))], 0)
    w = w.transpose(0, 4, 3, 1, 6, 5, 7, 2, 8)
    return w.reshape(36 * coils, 6 * shards * coils)


def split(x):
    hi = x.astype(jnp.bfloat16)
    return hi, (x - hi.astype(jnp.float32)).astype(jnp.bfloat16)


def body(sizes, row, measured, mask, weights, out, x, xh, xl, wh, wl, r1, r2, rm,
         g_send, g_recv, z_send, z_recv, k_send, k_recv, m_send, m_recv):
    nz, nc = sizes
    planes, rows, lanes = measured.shape
    wide = lanes + LANES
    z, c, h = lax.axis_index("kz"), lax.axis_index("coil"), lax.axis_index("kx")
    mirror = {"kz": nz - 1 - z, "kx": 1 - h}

    barrier = pltpu.get_barrier_semaphore()
    for d in range(1, nc):
        pl.semaphore_signal(barrier, inc=1, device_id={"coil": lax.rem(c + d, nc)}, device_id_type=MESH)
    pl.semaphore_signal(barrier, inc=1, device_id={"kx": 1 - h}, device_id_type=MESH)
    pl.semaphore_signal(barrier, inc=1, device_id=mirror, device_id_type=MESH)

    for d in (1, nz - 1):
        pl.semaphore_signal(barrier, inc=1, device_id={"kz": lax.rem(z + d, nz)}, device_id_type=MESH)
    pl.semaphore_wait(barrier, nc + 3)

    lane = lax.broadcasted_iota(jnp.int32, (1, wide), 1)
    edge = lane - lanes - h * (LANES - row)
    keep = (lane < lanes) | ((edge >= 0) & (edge < row))
    column = lax.rem(lane, row)
    after, before = column > 0, column < row - 1
    flip = (lax.broadcasted_iota(jnp.int32, (LANES, LANES), 0)
            + lax.broadcasted_iota(jnp.int32, (LANES, LANES), 1) == LANES - 1)
    flip = flip.astype(jnp.float32).astype(jnp.bfloat16)

    def remote(src, dst, send, recv, device):
        return pltpu.make_async_remote_copy(
            src_ref=src, dst_ref=dst, send_sem=send, recv_sem=recv, device_id=device, device_id_type=MESH)

    for step in range(ITERS):
        xs = x.at[step]

        def fill(k, _):
            sampled = mask[k] == 1
            if step == 0:
                value = jnp.where(sampled, measured[k], 0.0)
            else:
                value = combine(step - 1, k, sampled)
            xs[k + 1, c, :, :lanes] = value
            return 0

        def combine(last, k, sampled):
            got = rm[last, planes - 1 - k]
            hi, lo = split(got)
            parts = []
            for q in range(lanes // LANES):
                s = slice(lanes - (q + 1) * LANES, lanes - q * LANES)
                parts.append(jnp.dot(hi[:, s], flip, preferred_element_type=jnp.float32)
                             + jnp.dot(lo[:, s], flip, preferred_element_type=jnp.float32))
            return jnp.where(sampled, measured[k], r1[k] + jnp.concatenate(parts, 1))

        lax.fori_loop(0, planes, fill, 0)

        @pl.when(z == 0)
        def _():
            xs[0, :, :, :lanes] = jnp.zeros((nc, rows, lanes), jnp.float32)

        @pl.when(z == nz - 1)
        def _():
            xs[planes + 1, :, :, :lanes] = jnp.zeros((nc, rows, lanes), jnp.float32)

        if step == 0:
            wh[...], wl[...] = split(weights[...])

        own = xs.at[pl.ds(1, planes), c, :, pl.ds(0, lanes)]
        gathers = [remote(own, own, g_send.at[step, d - 1], g_recv.at[step, d - 1],
                          {"coil": lax.rem(c + d, nc)}) for d in range(1, nc)]
        for copy in gathers:
            copy.start()
        for copy in gathers:
            copy.wait()

        down = remote(xs.at[1, :, :, pl.ds(0, lanes)], xs.at[planes + 1, :, :, pl.ds(0, lanes)],
                      z_send.at[step, 0], z_recv.at[step, 0], {"kz": lax.max(z - 1, 0)})
        up = remote(xs.at[planes, :, :, pl.ds(0, lanes)], xs.at[0, :, :, pl.ds(0, lanes)],
                    z_send.at[step, 1], z_recv.at[step, 1], {"kz": lax.min(z + 1, nz - 1)})

        @pl.when(z > 0)
        def _():
            down.start()

        @pl.when(z < nz - 1)
        def _():
            up.start()

        @pl.when(z > 0)
        def _():
            down.wait_send()
            up.wait_recv()

        @pl.when(z < nz - 1)
        def _():
            up.wait_send()
            down.wait_recv()

        near = pl.multiple_of((1 - h) * (lanes - LANES), LANES)
        side = remote(xs.at[:, :, :, pl.ds(near, LANES)], xs.at[:, :, :, pl.ds(lanes, LANES)],
                      k_send.at[step], k_recv.at[step], {"kx": 1 - h})
        side.start()
        side.wait()

        def divide(k, _):
            value = xs[k].reshape(nc * rows, wide)
            xh[k], xl[k] = split(jnp.where(keep, value, 0.0))
            return 0

        lax.fori_loop(0, planes + 2, divide, 0)

        def send(k):
            return remote(r2.at[step, k], rm.at[step, k], m_send.at[step, k], m_recv.at[step, k], mirror)

        def convolve(k, _):
            hi = xh[pl.ds(k, 3)].reshape(-1, wide)
            lo = xl[pl.ds(k, 3)].reshape(-1, wide)
            results = []
            for v in (1, 0):
                w = slice(v * 9 * rows, (v + 1) * 9 * rows)
                p = (jnp.dot(wh[w], hi, preferred_element_type=jnp.float32)
                     + jnp.dot(wh[w], lo, preferred_element_type=jnp.float32)
                     + jnp.dot(wl[w], hi, preferred_element_type=jnp.float32))
                total = None
                for b in (1, 0, 2):
                    t = p[(3 * b + 1) * rows:(3 * b + 2) * rows]
                    t = t + pltpu.roll(p[3 * b * rows:(3 * b + 1) * rows], row, 1)
                    t = t + pltpu.roll(p[(3 * b + 2) * rows:(3 * b + 3) * rows], wide - row, 1)
                    if b == 0:
                        t = jnp.where(after, pltpu.roll(t, 1, 1), 0.0)
                    if b == 2:
                        t = jnp.where(before, pltpu.roll(t, wide - 1, 1), 0.0)
                    total = t if total is None else total + t
                results.append(total[:, :lanes])
            r2[step, k] = results[0]
            r1[k] = results[1]

            @pl.when(k > 0)
            def _():
                send(k - 1).start()

            return 0

        lax.fori_loop(0, planes, convolve, 0)
        send(planes - 1).start()

        def finish(k, _):
            send(k).wait()
            return 0

        lax.fori_loop(0, planes, finish, 0)

    def last(k, _):
        out[k] = combine(ITERS - 1, k, mask[k] == 1)
        return 0

    lax.fori_loop(0, planes, last, 0)


def on_device(sizes, measured, mask, kernel):
    nz, nc = sizes
    _, coils, depth_x, planes, row = measured.shape
    rows, lanes = 2 * coils, depth_x * row
    wide = lanes + LANES
    weights = build_weights(kernel, nc)
    flat = measured.transpose(3, 0, 1, 2, 4).reshape(planes, rows, lanes)
    sampled = mask.transpose(1, 0, 2).reshape(planes, 1, lanes)
    vmem = pl.BlockSpec(memory_space=pltpu.VMEM)
    dma = pltpu.SemaphoreType.DMA
    result = pl.pallas_call(
        functools.partial(body, sizes, row),
        out_shape=jax.ShapeDtypeStruct((planes, rows, lanes), jnp.float32),
        in_specs=[vmem] * 3,
        out_specs=vmem,
        scratch_shapes=[
            pltpu.VMEM((ITERS, planes + 2, nc, rows, wide), jnp.float32),
            pltpu.VMEM((planes + 2, nc * rows, wide), jnp.bfloat16),
            pltpu.VMEM((planes + 2, nc * rows, wide), jnp.bfloat16),
            pltpu.VMEM(weights.shape, jnp.bfloat16),
            pltpu.VMEM(weights.shape, jnp.bfloat16),
            pltpu.VMEM((planes, rows, lanes), jnp.float32),
            pltpu.VMEM((ITERS, planes, rows, lanes), jnp.float32),
            pltpu.VMEM((ITERS, planes, rows, lanes), jnp.float32),
            dma((ITERS, nc - 1)), dma((ITERS, nc - 1)),
            dma((ITERS, 2)), dma((ITERS, 2)),
            dma((ITERS,)), dma((ITERS,)),
            dma((ITERS, planes)), dma((ITERS, planes)),
        ],
        compiler_params=pltpu.CompilerParams(collective_id=0, has_side_effects=True),
    )(flat, sampled, weights)
    result = result.reshape(planes, 2, coils, depth_x, row)
    return result.transpose(1, 2, 3, 0, 4)


def solution(mesh):
    placed = (
        P(None, ("grp", "coil"), "kx", "kz", None),
        P(("grp", "kx"), "kz", None),
        P(None, None, "coil", None),
    )
    return jax.shard_map(
        functools.partial(on_device, (mesh.shape["kz"], mesh.shape["coil"])),
        mesh=mesh,
        in_specs=placed,
        out_specs=P(None, ("grp", "coil"), "kx", "kz", None),
        check_vma=False,
    )
```

```python
import functools

import jax
import jax.numpy as jnp
from jax import lax
from jax.experimental import pallas as pl
from jax.experimental.pallas import tpu as pltpu
from jax.sharding import PartitionSpec as P

ITERS = 2
LANES = 128
MESH = pl.DeviceIdType.MESH


def order(n, count, turn):
    odd = (n + turn) % 2
    return (1 - odd) * (count // 2 - 1 - n // 2) + odd * (count // 2 + n // 2)


def place_weights(kernel, shards, wf, target, low):
    taps, _, coils, inputs = kernel.shape
    width = 2 * inputs
    half = inputs // 2
    shape = (inputs, 2 * width)
    d = lax.broadcasted_iota(jnp.int32, shape, 0)
    q = lax.broadcasted_iota(jnp.int32, shape, 1)
    v, po = q // width, (q // inputs) % 2
    at = q % inputs
    pi, source = (at // coils) % 2, v * half + (at // (2 * coils)) * coils + at % coils
    hit = d == source
    real = jnp.where(hit & (po == pi), jnp.where((v == 1) & (po == 1), -1.0, 1.0), 0.0).astype(jnp.bfloat16)
    imag = jnp.where(hit & (po != pi), jnp.where((v == 0) & (po == 0), -1.0, 1.0), 0.0).astype(jnp.bfloat16)
    picked = (jnp.dot(split(kernel[:, 0].reshape(taps * coils, inputs))[low], real, preferred_element_type=jnp.float32)
              + jnp.dot(split(kernel[:, 1].reshape(taps * coils, inputs))[low], imag, preferred_element_type=jnp.float32))
    for v in range(2):
        for b in range(3):
            for a in range(3):
                for po in range(2):
                    parts = []
                    for e in range(3):
                        t = 9 * a + 3 * b + e
                        t = taps - 1 - t if v else t
                        parts.append(picked[t * coils:(t + 1) * coils, (2 * v + po) * inputs:(2 * v + po + 1) * inputs])
                    first = (((v * 3 + b) * 3 + a) * 2 + po) * coils
                    wf[first:first + coils, :] = jnp.concatenate(parts, 1)
    target[...] = wf[...].astype(jnp.bfloat16)


def split(x):
    hi = x.astype(jnp.bfloat16)
    return hi, (x - hi.astype(jnp.float32)).astype(jnp.bfloat16)


def body(sizes, row, measured, mask, kernel, out, x, xh, xl, wf, wh, wl, r1, r2, rm,
         g_send, g_recv, z_send, z_recv, k_send, k_recv, m_send, m_recv):
    nz, nc = sizes
    planes, rows, lanes = measured.shape
    wide = lanes + LANES
    z, c, h = lax.axis_index("kz"), lax.axis_index("coil"), lax.axis_index("kx")
    mirror = {"kz": nz - 1 - z, "kx": 1 - h}

    barrier = pltpu.get_barrier_semaphore()
    for d in range(1, nc):
        pl.semaphore_signal(barrier, inc=1, device_id={"coil": lax.rem(c + d, nc)}, device_id_type=MESH)
    pl.semaphore_signal(barrier, inc=1, device_id={"kx": 1 - h}, device_id_type=MESH)
    pl.semaphore_signal(barrier, inc=1, device_id=mirror, device_id_type=MESH)

    for d in (1, nz - 1):
        pl.semaphore_signal(barrier, inc=1, device_id={"kz": lax.rem(z + d, nz)}, device_id_type=MESH)
    pl.semaphore_wait(barrier, nc + 3)

    lane = lax.broadcasted_iota(jnp.int32, (1, wide), 1)
    edge = lane - lanes - h * (LANES - row)
    keep = (lane < lanes) | ((edge >= 0) & (edge < row))
    column = lax.rem(lane, row)
    after, before = column > 0, column < row - 1
    flip = (lax.broadcasted_iota(jnp.int32, (LANES, LANES), 0)
            + lax.broadcasted_iota(jnp.int32, (LANES, LANES), 1) == LANES - 1)
    flip = flip.astype(jnp.float32).astype(jnp.bfloat16)

    def remote(src, dst, send, recv, device):
        return pltpu.make_async_remote_copy(
            src_ref=src, dst_ref=dst, send_sem=send, recv_sem=recv, device_id=device, device_id_type=MESH)

    slots = planes + 2

    def combine(step, k):
        sampled = mask[k] == 1
        hi, lo = split(rm[step, k])
        parts = []
        for q in range(lanes // LANES):
            s = slice(lanes - (q + 1) * LANES, lanes - q * LANES)
            parts.append(jnp.dot(hi[:, s], flip, preferred_element_type=jnp.float32)
                         + jnp.dot(lo[:, s], flip, preferred_element_type=jnp.float32))
        return jnp.where(sampled, measured[k], r1[k] + jnp.concatenate(parts, 1))

    def gather(step, slot, d):
        own = x.at[step, slot, c, :, pl.ds(0, lanes)]
        return remote(own, own, g_send.at[step, d - 1, slot], g_recv.at[step, d - 1, slot],
                      {"coil": lax.rem(c + d, nc)})

    def outer(step):
        down = remote(x.at[step, 1, c, :, pl.ds(0, lanes)], x.at[step, planes + 1, c, :, pl.ds(0, lanes)],
                      z_send.at[step, 0], z_recv.at[step, 0], {"kz": lax.max(z - 1, 0)})
        up = remote(x.at[step, planes, c, :, pl.ds(0, lanes)], x.at[step, 0, c, :, pl.ds(0, lanes)],
                    z_send.at[step, 1], z_recv.at[step, 1], {"kz": lax.min(z + 1, nz - 1)})
        return down, up

    def side(step, slot):
        near = pl.multiple_of((1 - h) * (lanes - LANES), LANES)
        return remote(x.at[step, slot, :, :, pl.ds(near, LANES)], x.at[step, slot, :, :, pl.ds(lanes, LANES)],
                      k_send.at[step, slot], k_recv.at[step, slot], {"kx": 1 - h})

    def send(step, k):
        return remote(r2.at[step, k], rm.at[step, planes - 1 - k], m_send.at[step, k],
                      m_recv.at[step, planes - 1 - k], mirror)

    def receive(step, k):
        remote(r2.at[step, planes - 1 - k], rm.at[step, k], m_send.at[step, planes - 1 - k],
               m_recv.at[step, k], mirror).wait_recv()

    def start_outer(step):
        down, up = outer(step)

        @pl.when(z > 0)
        def _():
            down.start()

        @pl.when(z < nz - 1)
        def _():
            up.start()

    def wait_outer(step):
        down, up = outer(step)

        @pl.when(z > 0)
        def _():
            down.wait_send()
            up.wait_recv()

        @pl.when(z < nz - 1)
        def _():
            up.wait_send()
            down.wait_recv()

    def start_gather(step, n):
        for d in range(1, nc):
            gather(step, order(n, slots, step), d).start()

    def wait_gather(step, n):
        slot = order(n, slots, step)
        for d in range(1, nc):
            gather(step, slot, d).wait_recv()
        side(step, slot).start()

    def divide(step, n):
        slot = order(n, slots, step)
        side(step, slot).wait_recv()
        value = x[step, slot].reshape(nc * rows, wide)
        xh[slot], xl[slot] = split(jnp.where(keep, value, 0.0))

    def convolve(step, n):
        k = order(n, slots, step) - 1
        hi = xh[pl.ds(k, 3)].reshape(-1, wide)
        lo = xl[pl.ds(k, 3)].reshape(-1, wide)
        results = []
        for v in (1, 0):
            w = slice(v * 9 * rows, (v + 1) * 9 * rows)
            p = (jnp.dot(wh[w], hi, preferred_element_type=jnp.float32)
                 + jnp.dot(wh[w], lo, preferred_element_type=jnp.float32)
                 + jnp.dot(wl[w], hi, preferred_element_type=jnp.float32))
            total = None
            for b in (1, 0, 2):
                t = p[(3 * b + 1) * rows:(3 * b + 2) * rows]
                t = t + pltpu.roll(p[3 * b * rows:(3 * b + 1) * rows], row, 1)
                t = t + pltpu.roll(p[(3 * b + 2) * rows:(3 * b + 3) * rows], wide - row, 1)
                if b == 0:
                    t = jnp.where(after, pltpu.roll(t, 1, 1), 0.0)
                if b == 2:
                    t = jnp.where(before, pltpu.roll(t, wide - 1, 1), 0.0)
                total = t if total is None else total + t
            results.append(total[:, :lanes])
            if v:
                r2[step, k] = results[0]
        r1[k] = results[1]
        send(step, k).start()

    for step in range(ITERS):
        @pl.when(z == 0)
        def _():
            x[step, 0, c, :, :lanes] = jnp.zeros((rows, lanes), jnp.float32)

        @pl.when(z == nz - 1)
        def _():
            x[step, planes + 1, c, :, :lanes] = jnp.zeros((rows, lanes), jnp.float32)

    def first(k, _):
        x[0, k + 1, c, :, :lanes] = jnp.where(mask[k] == 1, measured[k], 0.0)
        return 0

    lax.fori_loop(0, planes, first, 0)
    start_outer(0)

    def first_gather(n, _):
        start_gather(0, n)
        return 0

    lax.fori_loop(0, planes, first_gather, 0)
    place_weights(kernel, nc, wf, wh, 0)
    wait_outer(0)
    lax.fori_loop(planes, slots, first_gather, 0)
    place_weights(kernel, nc, wf, wl, 1)

    for step in range(ITERS):
        lag = 1 if step else 0

        def stage(n, _):
            if step:
                @pl.when(n < planes)
                def _():
                    k = order(n, slots, step) - 1
                    receive(step - 1, k)
                    x[step, k + 1, c, :, :lanes] = combine(step - 1, k)

                @pl.when(n == planes)
                def _():
                    start_outer(step)
                    wait_outer(step)

            @pl.when((n >= 1 + lag) & (n < slots + 1 + lag))
            def _():
                divide(step, n - 1 - lag)

            if step:
                @pl.when(n < slots)
                def _():
                    start_gather(step, n)

            @pl.when((n >= lag) & (n < slots + lag))
            def _():
                wait_gather(step, n - lag)

            @pl.when(n >= 3 + lag)
            def _():
                convolve(step, n - 3 - lag)

            return 0

        lax.fori_loop(0, planes + 3 + lag, stage, 0)

    def last(n, _):
        k = order(n, slots, ITERS) - 1
        receive(ITERS - 1, k)
        out[k] = combine(ITERS - 1, k)
        return 0

    lax.fori_loop(0, planes, last, 0)

    for step in range(ITERS):
        def sent(slot, _):
            for d in range(1, nc):
                gather(step, slot, d).wait_send()
            side(step, slot).wait_send()
            return 0

        lax.fori_loop(0, slots, sent, 0)

        def mirrored(k, _):
            send(step, k).wait_send()
            return 0

        lax.fori_loop(0, planes, mirrored, 0)


def on_device(sizes, measured, mask, kernel):
    nz, nc = sizes
    _, coils, depth_x, planes, row = measured.shape
    rows, lanes = 2 * coils, depth_x * row
    wide = lanes + LANES
    flat = measured.transpose(3, 0, 1, 2, 4).reshape(planes, rows, lanes)
    sampled = mask.transpose(1, 0, 2).reshape(planes, 1, lanes)
    weights = (18 * rows, 3 * nc * rows)
    vmem = pl.BlockSpec(memory_space=pltpu.VMEM)
    dma = pltpu.SemaphoreType.DMA
    result = pl.pallas_call(
        functools.partial(body, sizes, row),
        out_shape=jax.ShapeDtypeStruct((planes, rows, lanes), jnp.float32),
        in_specs=[vmem] * 3,
        out_specs=vmem,
        scratch_shapes=[
            pltpu.VMEM((ITERS, planes + 2, nc, rows, wide), jnp.float32),
            pltpu.VMEM((planes + 2, nc * rows, wide), jnp.bfloat16),
            pltpu.VMEM((planes + 2, nc * rows, wide), jnp.bfloat16),
            pltpu.VMEM(weights, jnp.float32),
            pltpu.VMEM(weights, jnp.bfloat16),
            pltpu.VMEM(weights, jnp.bfloat16),
            pltpu.VMEM((planes, rows, lanes), jnp.float32),
            pltpu.VMEM((ITERS, planes, rows, lanes), jnp.float32),
            pltpu.VMEM((ITERS, planes, rows, lanes), jnp.float32),
            dma((ITERS, nc - 1, planes + 2)), dma((ITERS, nc - 1, planes + 2)),
            dma((ITERS, 2)), dma((ITERS, 2)),
            dma((ITERS, planes + 2)), dma((ITERS, planes + 2)),
            dma((ITERS, planes)), dma((ITERS, planes)),
        ],
        compiler_params=pltpu.CompilerParams(collective_id=0, has_side_effects=True),
    )(flat, sampled, kernel)
    result = result.reshape(planes, 2, coils, depth_x, row)
    return result.transpose(1, 2, 3, 0, 4)


def solution(mesh):
    placed = (
        P(None, ("grp", "coil"), "kx", "kz", None),
        P(("grp", "kx"), "kz", None),
        P(None, None, "coil", None),
    )
    return jax.shard_map(
        functools.partial(on_device, (mesh.shape["kz"], mesh.shape["coil"])),
        mesh=mesh,
        in_specs=placed,
        out_specs=P(None, ("grp", "coil"), "kx", "kz", None),
        check_vma=False,
    )
```

```python
import functools

import jax
import jax.numpy as jnp
from jax import lax
from jax.experimental import pallas as pl
from jax.experimental.pallas import tpu as pltpu
from jax.sharding import PartitionSpec as P

ITERS = 2
LANES = 128
MESH = pl.DeviceIdType.MESH


def order(n, count, turn):
    odd = (n + turn) % 2
    return (1 - odd) * (count // 2 - 1 - n // 2) + odd * (count // 2 + n // 2)


def place_weights(kernel, shards, wf, target, low):
    taps, _, coils, inputs = kernel.shape
    width = 2 * inputs
    half = inputs // 2
    shape = (inputs, 2 * width)
    d = lax.broadcasted_iota(jnp.int32, shape, 0)
    q = lax.broadcasted_iota(jnp.int32, shape, 1)
    v, po = q // width, (q // inputs) % 2
    at = q % inputs
    pi, source = (at // coils) % 2, v * half + (at // (2 * coils)) * coils + at % coils
    hit = d == source
    real = jnp.where(hit & (po == pi), jnp.where((v == 1) & (po == 1), -1.0, 1.0), 0.0).astype(jnp.bfloat16)
    imag = jnp.where(hit & (po != pi), jnp.where((v == 0) & (po == 0), -1.0, 1.0), 0.0).astype(jnp.bfloat16)
    picked = (jnp.dot(split(kernel[:, 0].reshape(taps * coils, inputs))[low], real, preferred_element_type=jnp.float32)
              + jnp.dot(split(kernel[:, 1].reshape(taps * coils, inputs))[low], imag, preferred_element_type=jnp.float32))
    for v in range(2):
        for b in range(3):
            for a in range(3):
                for po in range(2):
                    parts = []
                    for e in range(3):
                        t = 9 * a + 3 * b + e
                        t = taps - 1 - t if v else t
                        parts.append(picked[t * coils:(t + 1) * coils, (2 * v + po) * inputs:(2 * v + po + 1) * inputs])
                    first = (((v * 3 + b) * 3 + a) * 2 + po) * coils
                    wf[first:first + coils, :] = jnp.concatenate(parts, 1)
    target[...] = wf[...].astype(jnp.bfloat16)


def split(x):
    hi = x.astype(jnp.bfloat16)
    return hi, (x - hi.astype(jnp.float32)).astype(jnp.bfloat16)


def body(sizes, row, measured, mask, kernel, out, x, xh, xl, wf, wh, wl, r1, r2, rm,
         g_send, g_recv, z_send, z_recv, k_send, k_recv, m_send, m_recv):
    nz, nc = sizes
    planes, rows, lanes = measured.shape
    wide = lanes + LANES
    z, c, h = lax.axis_index("kz"), lax.axis_index("coil"), lax.axis_index("kx")
    mirror = {"kz": nz - 1 - z, "kx": 1 - h}

    barrier = pltpu.get_barrier_semaphore()
    for d in range(1, nc):
        pl.semaphore_signal(barrier, inc=1, device_id={"coil": lax.rem(c + d, nc)}, device_id_type=MESH)
    pl.semaphore_signal(barrier, inc=1, device_id={"kx": 1 - h}, device_id_type=MESH)
    pl.semaphore_signal(barrier, inc=1, device_id=mirror, device_id_type=MESH)

    for d in (1, nz - 1):
        pl.semaphore_signal(barrier, inc=1, device_id={"kz": lax.rem(z + d, nz)}, device_id_type=MESH)
    pl.semaphore_wait(barrier, nc + 3)

    lane = lax.broadcasted_iota(jnp.int32, (1, wide), 1)
    edge = lane - lanes - h * (LANES - row)
    keep = (lane < lanes) | ((edge >= 0) & (edge < row))
    column = lax.rem(lane, row)
    after, before = column > 0, column < row - 1
    flip = (lax.broadcasted_iota(jnp.int32, (LANES, LANES), 0)
            + lax.broadcasted_iota(jnp.int32, (LANES, LANES), 1) == LANES - 1)
    flip = flip.astype(jnp.float32).astype(jnp.bfloat16)

    def remote(src, dst, send, recv, device):
        return pltpu.make_async_remote_copy(
            src_ref=src, dst_ref=dst, send_sem=send, recv_sem=recv, device_id=device, device_id_type=MESH)

    slots = planes + 2

    def combine(step, k):
        sampled = mask[k] == 1
        hi, lo = split(rm[step, k])
        parts = []
        for q in range(lanes // LANES):
            s = slice(lanes - (q + 1) * LANES, lanes - q * LANES)
            parts.append(jnp.dot(hi[:, s], flip, preferred_element_type=jnp.float32)
                         + jnp.dot(lo[:, s], flip, preferred_element_type=jnp.float32))
        return jnp.where(sampled, measured[k], r1[k] + jnp.concatenate(parts, 1))

    def gather(step, slot, d):
        own = x.at[step, slot, c, :, pl.ds(0, lanes)]
        return remote(own, own, g_send.at[step, d - 1, slot], g_recv.at[step, d - 1, slot],
                      {"coil": lax.rem(c + d, nc)})

    def outer(step):
        down = remote(x.at[step, 1, c, :, pl.ds(0, lanes)], x.at[step, planes + 1, c, :, pl.ds(0, lanes)],
                      z_send.at[step, 0], z_recv.at[step, 0], {"kz": lax.max(z - 1, 0)})
        up = remote(x.at[step, planes, c, :, pl.ds(0, lanes)], x.at[step, 0, c, :, pl.ds(0, lanes)],
                    z_send.at[step, 1], z_recv.at[step, 1], {"kz": lax.min(z + 1, nz - 1)})
        return down, up

    def side(step, slot):
        near = pl.multiple_of((1 - h) * (lanes - LANES), LANES)
        return remote(x.at[step, slot, :, :, pl.ds(near, LANES)], x.at[step, slot, :, :, pl.ds(lanes, LANES)],
                      k_send.at[step, slot], k_recv.at[step, slot], {"kx": 1 - h})

    def send(step, k):
        return remote(r2.at[step, k], rm.at[step, planes - 1 - k], m_send.at[step, k],
                      m_recv.at[step, planes - 1 - k], mirror)

    def receive(step, k):
        remote(r2.at[step, planes - 1 - k], rm.at[step, k], m_send.at[step, planes - 1 - k],
               m_recv.at[step, k], mirror).wait_recv()

    def start_outer(step):
        down, up = outer(step)

        @pl.when(z > 0)
        def _():
            down.start()

        @pl.when(z < nz - 1)
        def _():
            up.start()

    def wait_outer(step):
        down, up = outer(step)

        @pl.when(z > 0)
        def _():
            down.wait_send()
            up.wait_recv()

        @pl.when(z < nz - 1)
        def _():
            up.wait_send()
            down.wait_recv()

    def start_gather(step, n):
        for d in range(1, nc):
            gather(step, order(n, slots, step), d).start()

    def wait_gather(step, n):
        slot = order(n, slots, step)
        for d in range(1, nc):
            gather(step, slot, d).wait_recv()
        side(step, slot).start()

    def divide(step, n):
        slot = order(n, slots, step)
        side(step, slot).wait_recv()
        value = x[step, slot].reshape(nc * rows, wide)
        xh[slot], xl[slot] = split(jnp.where(keep, value, 0.0))

    def convolve(step, n):
        k = order(n, slots, step) - 1
        hi = xh[pl.ds(k, 3)].reshape(-1, wide)
        lo = xl[pl.ds(k, 3)].reshape(-1, wide)
        results = []
        for v in (1, 0):
            w = slice(v * 9 * rows, (v + 1) * 9 * rows)
            p = (jnp.dot(wh[w], hi, preferred_element_type=jnp.float32)
                 + jnp.dot(wh[w], lo, preferred_element_type=jnp.float32)
                 + jnp.dot(wl[w], hi, preferred_element_type=jnp.float32))
            total = None
            for b in (1, 0, 2):
                t = p[(3 * b + 1) * rows:(3 * b + 2) * rows]
                t = t + pltpu.roll(p[3 * b * rows:(3 * b + 1) * rows], row, 1)
                t = t + pltpu.roll(p[(3 * b + 2) * rows:(3 * b + 3) * rows], wide - row, 1)
                if b == 0:
                    t = jnp.where(after, pltpu.roll(t, 1, 1), 0.0)
                if b == 2:
                    t = jnp.where(before, pltpu.roll(t, wide - 1, 1), 0.0)
                total = t if total is None else total + t
            results.append(total[:, :lanes])
            if v:
                r2[step, k] = results[0]
        r1[k] = results[1]
        send(step, k).start()

    for step in range(ITERS):
        @pl.when(z == 0)
        def _():
            x[step, 0, c, :, :lanes] = jnp.zeros((rows, lanes), jnp.float32)

        @pl.when(z == nz - 1)
        def _():
            x[step, planes + 1, c, :, :lanes] = jnp.zeros((rows, lanes), jnp.float32)

    def first(k, _):
        x[0, k + 1, c, :, :lanes] = jnp.where(mask[k] == 1, measured[k], 0.0)
        return 0

    lax.fori_loop(0, planes, first, 0)
    start_outer(0)

    def first_gather(n, _):
        start_gather(0, n)
        return 0

    lax.fori_loop(0, planes, first_gather, 0)
    place_weights(kernel, nc, wf, wh, 0)
    wait_outer(0)
    lax.fori_loop(planes, slots, first_gather, 0)
    place_weights(kernel, nc, wf, wl, 1)

    def stage(n, _):
        @pl.when((n >= 1) & (n < slots + 1))
        def _():
            divide(0, n - 1)

        @pl.when(n < slots)
        def _():
            wait_gather(0, n)

        @pl.when(n >= 3)
        def _():
            convolve(0, n - 3)

        return 0

    lax.fori_loop(0, planes + 3, stage, 0)

    for step in range(1, ITERS):
        def again(n, _):
            @pl.when(n < planes)
            def _():
                k = order(n, slots, step) - 1
                receive(step - 1, k)
                x[step, k + 1, c, :, :lanes] = combine(step - 1, k)

            @pl.when(n >= 2)
            def _():
                divide(step, n - 2)

            @pl.when(n == planes - 1)
            def _():
                start_outer(step)

            @pl.when(n < planes)
            def _():
                start_gather(step, n)

            @pl.when((n >= 1) & (n < planes + 1))
            def _():
                wait_gather(step, n - 1)

            @pl.when(n >= 4)
            def _():
                convolve(step, n - 4)

            return 0

        lax.fori_loop(0, planes + 2, again, 0)
        wait_outer(step)
        for n in (planes, planes + 1):
            start_gather(step, n)
        for n in (planes, planes + 1):
            wait_gather(step, n)

        def rest(n, _):
            divide(step, n + 2)
            convolve(step, n)
            return 0

        lax.fori_loop(planes - 2, planes, rest, 0)

    def last(n, _):
        k = order(n, slots, ITERS) - 1
        receive(ITERS - 1, k)
        out[k] = combine(ITERS - 1, k)
        return 0

    lax.fori_loop(0, planes, last, 0)

    for step in range(ITERS):
        def sent(slot, _):
            for d in range(1, nc):
                gather(step, slot, d).wait_send()
            side(step, slot).wait_send()
            return 0

        lax.fori_loop(0, slots, sent, 0)

        def mirrored(k, _):
            send(step, k).wait_send()
            return 0

        lax.fori_loop(0, planes, mirrored, 0)


def on_device(sizes, measured, mask, kernel):
    nz, nc = sizes
    _, coils, depth_x, planes, row = measured.shape
    rows, lanes = 2 * coils, depth_x * row
    wide = lanes + LANES
    flat = measured.transpose(3, 0, 1, 2, 4).reshape(planes, rows, lanes)
    sampled = mask.transpose(1, 0, 2).reshape(planes, 1, lanes)
    weights = (18 * rows, 3 * nc * rows)
    vmem = pl.BlockSpec(memory_space=pltpu.VMEM)
    dma = pltpu.SemaphoreType.DMA
    result = pl.pallas_call(
        functools.partial(body, sizes, row),
        out_shape=jax.ShapeDtypeStruct((planes, rows, lanes), jnp.float32),
        in_specs=[vmem] * 3,
        out_specs=vmem,
        scratch_shapes=[
            pltpu.VMEM((ITERS, planes + 2, nc, rows, wide), jnp.float32),
            pltpu.VMEM((planes + 2, nc * rows, wide), jnp.bfloat16),
            pltpu.VMEM((planes + 2, nc * rows, wide), jnp.bfloat16),
            pltpu.VMEM(weights, jnp.float32),
            pltpu.VMEM(weights, jnp.bfloat16),
            pltpu.VMEM(weights, jnp.bfloat16),
            pltpu.VMEM((planes, rows, lanes), jnp.float32),
            pltpu.VMEM((ITERS, planes, rows, lanes), jnp.float32),
            pltpu.VMEM((ITERS, planes, rows, lanes), jnp.float32),
            dma((ITERS, nc - 1, planes + 2)), dma((ITERS, nc - 1, planes + 2)),
            dma((ITERS, 2)), dma((ITERS, 2)),
            dma((ITERS, planes + 2)), dma((ITERS, planes + 2)),
            dma((ITERS, planes)), dma((ITERS, planes)),
        ],
        compiler_params=pltpu.CompilerParams(collective_id=0, has_side_effects=True),
    )(flat, sampled, kernel)
    result = result.reshape(planes, 2, coils, depth_x, row)
    return result.transpose(1, 2, 3, 0, 4)


def solution(mesh):
    placed = (
        P(None, ("grp", "coil"), "kx", "kz", None),
        P(("grp", "kx"), "kz", None),
        P(None, None, "coil", None),
    )
    return jax.shard_map(
        functools.partial(on_device, (mesh.shape["kz"], mesh.shape["coil"])),
        mesh=mesh,
        in_specs=placed,
        out_specs=P(None, ("grp", "coil"), "kx", "kz", None),
        check_vma=False,
    )
```

```python
import functools

import jax
import jax.numpy as jnp
from jax import lax
from jax.experimental import pallas as pl
from jax.experimental.pallas import tpu as pltpu
from jax.sharding import PartitionSpec as P

ITERS = 2
LANES = 128
MESH = pl.DeviceIdType.MESH


def order(n, count, turn):
    odd = (n + turn) % 2
    return (1 - odd) * (count // 2 - 1 - n // 2) + odd * (count // 2 + n // 2)


def place_weights(kernel, shards, wf, target, low):
    taps, _, coils, inputs = kernel.shape
    width = 2 * inputs
    half = inputs // 2
    shape = (inputs, 2 * width)
    d = lax.broadcasted_iota(jnp.int32, shape, 0)
    q = lax.broadcasted_iota(jnp.int32, shape, 1)
    v, po = q // width, (q // inputs) % 2
    at = q % inputs
    pi, source = (at // coils) % 2, v * half + (at // (2 * coils)) * coils + at % coils
    hit = d == source
    real = jnp.where(hit & (po == pi), jnp.where((v == 1) & (po == 1), -1.0, 1.0), 0.0).astype(jnp.bfloat16)
    imag = jnp.where(hit & (po != pi), jnp.where((v == 0) & (po == 0), -1.0, 1.0), 0.0).astype(jnp.bfloat16)
    picked = (jnp.dot(split(kernel[:, 0].reshape(taps * coils, inputs))[low], real, preferred_element_type=jnp.float32)
              + jnp.dot(split(kernel[:, 1].reshape(taps * coils, inputs))[low], imag, preferred_element_type=jnp.float32))
    for v in range(2):
        for b in range(3):
            for a in range(3):
                for po in range(2):
                    parts = []
                    for e in range(3):
                        t = 9 * a + 3 * b + e
                        t = taps - 1 - t if v else t
                        parts.append(picked[t * coils:(t + 1) * coils, (2 * v + po) * inputs:(2 * v + po + 1) * inputs])
                    first = (((v * 3 + b) * 3 + a) * 2 + po) * coils
                    wf[first:first + coils, :] = jnp.concatenate(parts, 1)
    target[...] = wf[...].astype(jnp.bfloat16)


def split(x):
    hi = x.astype(jnp.bfloat16)
    return hi, (x - hi.astype(jnp.float32)).astype(jnp.bfloat16)


def body(sizes, row, measured, mask, kernel, out, x, xh, xl, wf, wh, wl, r1, r2, rm,
         g_send, g_recv, z_send, z_recv, k_send, k_recv, m_send, m_recv):
    nz, nc = sizes
    planes, rows, lanes = measured.shape
    wide = lanes + LANES
    z, c, h = lax.axis_index("kz"), lax.axis_index("coil"), lax.axis_index("kx")
    mirror = {"kz": nz - 1 - z, "kx": 1 - h}

    barrier = pltpu.get_barrier_semaphore()
    for d in range(1, nc):
        pl.semaphore_signal(barrier, inc=1, device_id={"coil": lax.rem(c + d, nc)}, device_id_type=MESH)
    pl.semaphore_signal(barrier, inc=1, device_id={"kx": 1 - h}, device_id_type=MESH)
    pl.semaphore_signal(barrier, inc=1, device_id=mirror, device_id_type=MESH)

    for d in (1, nz - 1):
        pl.semaphore_signal(barrier, inc=1, device_id={"kz": lax.rem(z + d, nz)}, device_id_type=MESH)
    pl.semaphore_wait(barrier, nc + 3)

    lane = lax.broadcasted_iota(jnp.int32, (1, wide), 1)
    edge = lane - lanes - h * (LANES - row)
    keep = (lane < lanes) | ((edge >= 0) & (edge < row))
    column = lax.rem(lane, row)
    after, before = column > 0, column < row - 1
    flip = (lax.broadcasted_iota(jnp.int32, (LANES, LANES), 0)
            + lax.broadcasted_iota(jnp.int32, (LANES, LANES), 1) == LANES - 1)
    flip = flip.astype(jnp.float32).astype(jnp.bfloat16)

    def remote(src, dst, send, recv, device):
        return pltpu.make_async_remote_copy(
            src_ref=src, dst_ref=dst, send_sem=send, recv_sem=recv, device_id=device, device_id_type=MESH)

    slots = planes + 2

    def combine(step, k):
        sampled = mask[k] == 1
        hi, lo = split(rm[step, k])
        parts = []
        for q in range(lanes // LANES):
            s = slice(lanes - (q + 1) * LANES, lanes - q * LANES)
            parts.append(jnp.dot(hi[:, s], flip, preferred_element_type=jnp.float32)
                         + jnp.dot(lo[:, s], flip, preferred_element_type=jnp.float32))
        return jnp.where(sampled, measured[k], r1[k] + jnp.concatenate(parts, 1))

    def gather(step, slot, d):
        own = x.at[step, slot, c, :, pl.ds(0, lanes)]
        return remote(own, own, g_send.at[step, d - 1, slot], g_recv.at[step, d - 1, slot],
                      {"coil": lax.rem(c + d, nc)})

    def outer(step):
        down = remote(x.at[step, 1, c, :, pl.ds(0, lanes)], x.at[step, planes + 1, c, :, pl.ds(0, lanes)],
                      z_send.at[step, 0], z_recv.at[step, 0], {"kz": lax.max(z - 1, 0)})
        up = remote(x.at[step, planes, c, :, pl.ds(0, lanes)], x.at[step, 0, c, :, pl.ds(0, lanes)],
                    z_send.at[step, 1], z_recv.at[step, 1], {"kz": lax.min(z + 1, nz - 1)})
        return down, up

    def side(step, slot):
        near = pl.multiple_of((1 - h) * (lanes - LANES), LANES)
        return remote(x.at[step, slot, :, :, pl.ds(near, LANES)], x.at[step, slot, :, :, pl.ds(lanes, LANES)],
                      k_send.at[step, slot], k_recv.at[step, slot], {"kx": 1 - h})

    def send(step, k):
        return remote(r2.at[step, k], rm.at[step, planes - 1 - k], m_send.at[step, k],
                      m_recv.at[step, planes - 1 - k], mirror)

    def receive(step, k):
        remote(r2.at[step, planes - 1 - k], rm.at[step, k], m_send.at[step, planes - 1 - k],
               m_recv.at[step, k], mirror).wait_recv()

    def start_outer(step):
        down, up = outer(step)

        @pl.when(z > 0)
        def _():
            down.start()

        @pl.when(z < nz - 1)
        def _():
            up.start()

    def wait_outer(step):
        down, up = outer(step)

        @pl.when(z > 0)
        def _():
            down.wait_send()
            up.wait_recv()

        @pl.when(z < nz - 1)
        def _():
            up.wait_send()
            down.wait_recv()

    def start_gather(step, n):
        for d in range(1, nc):
            gather(step, order(n, slots, step), d).start()

    def wait_gather(step, n):
        slot = order(n, slots, step)
        for d in range(1, nc):
            gather(step, slot, d).wait_recv()
        side(step, slot).start()

    def divide(step, n):
        slot = order(n, slots, step)
        side(step, slot).wait_recv()
        value = x[step, slot].reshape(nc * rows, wide)
        xh[slot], xl[slot] = split(jnp.where(keep, value, 0.0))

    def convolve(step, n):
        k = order(n, slots, step) - 1
        hi = xh[pl.ds(k, 3)].reshape(-1, wide)
        lo = xl[pl.ds(k, 3)].reshape(-1, wide)
        results = []
        for v in (1, 0):
            w = slice(v * 9 * rows, (v + 1) * 9 * rows)
            p = (jnp.dot(wh[w], hi, preferred_element_type=jnp.float32)
                 + jnp.dot(wh[w], lo, preferred_element_type=jnp.float32)
                 + jnp.dot(wl[w], hi, preferred_element_type=jnp.float32))
            total = None
            for b in (1, 0, 2):
                t = p[(3 * b + 1) * rows:(3 * b + 2) * rows]
                t = t + pltpu.roll(p[3 * b * rows:(3 * b + 1) * rows], row, 1)
                t = t + pltpu.roll(p[(3 * b + 2) * rows:(3 * b + 3) * rows], wide - row, 1)
                if b == 0:
                    t = jnp.where(after, pltpu.roll(t, 1, 1), 0.0)
                if b == 2:
                    t = jnp.where(before, pltpu.roll(t, wide - 1, 1), 0.0)
                total = t if total is None else total + t
            results.append(total[:, :lanes])
            if v:
                r2[step, k] = results[0]
        r1[k] = results[1]
        send(step, k).start()

    for step in range(ITERS):
        @pl.when(z == 0)
        def _():
            x[step, 0, c, :, :lanes] = jnp.zeros((rows, lanes), jnp.float32)

        @pl.when(z == nz - 1)
        def _():
            x[step, planes + 1, c, :, :lanes] = jnp.zeros((rows, lanes), jnp.float32)

    def first(k, _):
        x[0, k + 1, c, :, :lanes] = jnp.where(mask[k] == 1, measured[k], 0.0)
        return 0

    lax.fori_loop(0, planes, first, 0)
    start_outer(0)

    def first_gather(n, _):
        start_gather(0, n)
        return 0

    lax.fori_loop(0, planes, first_gather, 0)
    place_weights(kernel, nc, wf, wh, 0)
    wait_outer(0)
    lax.fori_loop(planes, slots, first_gather, 0)
    for n in (0, 1):
        wait_gather(0, n)
    place_weights(kernel, nc, wf, wl, 1)

    def stage(n, _):
        @pl.when(n < slots + 2)
        def _():
            divide(0, n - 2)

        @pl.when(n >= 4)
        def _():
            convolve(0, n - 4)

        @pl.when(n < slots)
        def _():
            wait_gather(0, n)

        return 0

    lax.fori_loop(2, planes + 4, stage, 0)

    for step in range(1, ITERS):
        def again(n, _):
            @pl.when(n < planes)
            def _():
                k = order(n, slots, step) - 1
                receive(step - 1, k)
                x[step, k + 1, c, :, :lanes] = combine(step - 1, k)

            @pl.when(n >= 2)
            def _():
                divide(step, n - 2)

            @pl.when(n == planes - 1)
            def _():
                start_outer(step)

            @pl.when(n < planes)
            def _():
                start_gather(step, n)

            @pl.when((n >= 1) & (n < planes + 1))
            def _():
                wait_gather(step, n - 1)

            @pl.when(n >= 4)
            def _():
                convolve(step, n - 4)

            return 0

        lax.fori_loop(0, planes + 2, again, 0)
        wait_outer(step)
        for n in (planes, planes + 1):
            start_gather(step, n)
        for n in (planes, planes + 1):
            wait_gather(step, n)

        def rest(n, _):
            divide(step, n + 2)
            convolve(step, n)
            return 0

        lax.fori_loop(planes - 2, planes, rest, 0)

    def last(n, _):
        k = order(n, slots, ITERS) - 1
        receive(ITERS - 1, k)
        out[k] = combine(ITERS - 1, k)
        return 0

    lax.fori_loop(0, planes, last, 0)

    for step in range(ITERS):
        def sent(slot, _):
            for d in range(1, nc):
                gather(step, slot, d).wait_send()
            side(step, slot).wait_send()
            return 0

        lax.fori_loop(0, slots, sent, 0)

        def mirrored(k, _):
            send(step, k).wait_send()
            return 0

        lax.fori_loop(0, planes, mirrored, 0)


def on_device(sizes, measured, mask, kernel):
    nz, nc = sizes
    _, coils, depth_x, planes, row = measured.shape
    rows, lanes = 2 * coils, depth_x * row
    wide = lanes + LANES
    flat = measured.transpose(3, 0, 1, 2, 4).reshape(planes, rows, lanes)
    sampled = mask.transpose(1, 0, 2).reshape(planes, 1, lanes)
    weights = (18 * rows, 3 * nc * rows)
    vmem = pl.BlockSpec(memory_space=pltpu.VMEM)
    dma = pltpu.SemaphoreType.DMA
    result = pl.pallas_call(
        functools.partial(body, sizes, row),
        out_shape=jax.ShapeDtypeStruct((planes, rows, lanes), jnp.float32),
        in_specs=[vmem] * 3,
        out_specs=vmem,
        scratch_shapes=[
            pltpu.VMEM((ITERS, planes + 2, nc, rows, wide), jnp.float32),
            pltpu.VMEM((planes + 2, nc * rows, wide), jnp.bfloat16),
            pltpu.VMEM((planes + 2, nc * rows, wide), jnp.bfloat16),
            pltpu.VMEM(weights, jnp.float32),
            pltpu.VMEM(weights, jnp.bfloat16),
            pltpu.VMEM(weights, jnp.bfloat16),
            pltpu.VMEM((planes, rows, lanes), jnp.float32),
            pltpu.VMEM((ITERS, planes, rows, lanes), jnp.float32),
            pltpu.VMEM((ITERS, planes, rows, lanes), jnp.float32),
            dma((ITERS, nc - 1, planes + 2)), dma((ITERS, nc - 1, planes + 2)),
            dma((ITERS, 2)), dma((ITERS, 2)),
            dma((ITERS, planes + 2)), dma((ITERS, planes + 2)),
            dma((ITERS, planes)), dma((ITERS, planes)),
        ],
        compiler_params=pltpu.CompilerParams(collective_id=0, has_side_effects=True),
    )(flat, sampled, kernel)
    result = result.reshape(planes, 2, coils, depth_x, row)
    return result.transpose(1, 2, 3, 0, 4)


def solution(mesh):
    placed = (
        P(None, ("grp", "coil"), "kx", "kz", None),
        P(("grp", "kx"), "kz", None),
        P(None, None, "coil", None),
    )
    return jax.shard_map(
        functools.partial(on_device, (mesh.shape["kz"], mesh.shape["coil"])),
        mesh=mesh,
        in_specs=placed,
        out_specs=P(None, ("grp", "coil"), "kx", "kz", None),
        check_vma=False,
    )
```

```python
import functools

import jax
import jax.numpy as jnp
from jax import lax
from jax.experimental import pallas as pl
from jax.experimental.pallas import tpu as pltpu
from jax.sharding import PartitionSpec as P

ITERS = 2
LANES = 128
MESH = pl.DeviceIdType.MESH


def order(n, count, turn):
    odd = (n + turn) % 2
    return (1 - odd) * (count // 2 - 1 - n // 2) + odd * (count // 2 + n // 2)


def place_weights(kernel, shards, wf, target, low):
    taps, _, coils, inputs = kernel.shape
    width = 2 * inputs
    half = inputs // 2
    shape = (inputs, 2 * width)
    d = lax.broadcasted_iota(jnp.int32, shape, 0)
    q = lax.broadcasted_iota(jnp.int32, shape, 1)
    v, po = q // width, (q // inputs) % 2
    at = q % inputs
    pi, source = (at // coils) % 2, v * half + (at // (2 * coils)) * coils + at % coils
    hit = d == source
    real = jnp.where(hit & (po == pi), jnp.where((v == 1) & (po == 1), -1.0, 1.0), 0.0).astype(jnp.bfloat16)
    imag = jnp.where(hit & (po != pi), jnp.where((v == 0) & (po == 0), -1.0, 1.0), 0.0).astype(jnp.bfloat16)
    picked = (jnp.dot(split(kernel[:, 0].reshape(taps * coils, inputs))[low], real, preferred_element_type=jnp.float32)
              + jnp.dot(split(kernel[:, 1].reshape(taps * coils, inputs))[low], imag, preferred_element_type=jnp.float32))
    for v in range(2):
        for b in range(3):
            for a in range(3):
                for po in range(2):
                    parts = []
                    for e in range(3):
                        t = 9 * a + 3 * b + e
                        t = taps - 1 - t if v else t
                        parts.append(picked[t * coils:(t + 1) * coils, (2 * v + po) * inputs:(2 * v + po + 1) * inputs])
                    first = (((v * 3 + b) * 3 + a) * 2 + po) * coils
                    wf[first:first + coils, :] = jnp.concatenate(parts, 1)
    target[...] = wf[...].astype(jnp.bfloat16)


def split(x):
    hi = x.astype(jnp.bfloat16)
    return hi, (x - hi.astype(jnp.float32)).astype(jnp.bfloat16)


def body(sizes, row, measured, mask, kernel, out, x, xh, xl, wf, wh, wl, r1, r2, rm,
         g_send, g_recv, z_send, z_recv, k_send, k_recv, m_send, m_recv):
    nz, nc = sizes
    planes, rows, lanes = measured.shape
    wide = lanes + LANES
    z, c, h = lax.axis_index("kz"), lax.axis_index("coil"), lax.axis_index("kx")
    mirror = {"kz": nz - 1 - z, "kx": 1 - h}

    barrier = pltpu.get_barrier_semaphore()
    for d in range(1, nc):
        pl.semaphore_signal(barrier, inc=1, device_id={"coil": lax.rem(c + d, nc)}, device_id_type=MESH)
    pl.semaphore_signal(barrier, inc=1, device_id={"kx": 1 - h}, device_id_type=MESH)
    pl.semaphore_signal(barrier, inc=1, device_id=mirror, device_id_type=MESH)

    for d in (1, nz - 1):
        pl.semaphore_signal(barrier, inc=1, device_id={"kz": lax.rem(z + d, nz)}, device_id_type=MESH)
    pl.semaphore_wait(barrier, nc + 3)

    lane = lax.broadcasted_iota(jnp.int32, (1, wide), 1)
    edge = lane - lanes - h * (LANES - row)
    keep = (lane < lanes) | ((edge >= 0) & (edge < row))
    column = lax.rem(lane, row)
    after, before = column > 0, column < row - 1
    flip = (lax.broadcasted_iota(jnp.int32, (LANES, LANES), 0)
            + lax.broadcasted_iota(jnp.int32, (LANES, LANES), 1) == LANES - 1)
    flip = flip.astype(jnp.float32).astype(jnp.bfloat16)

    def remote(src, dst, send, recv, device):
        return pltpu.make_async_remote_copy(
            src_ref=src, dst_ref=dst, send_sem=send, recv_sem=recv, device_id=device, device_id_type=MESH)

    slots = planes + 2

    def combine(step, k):
        sampled = mask[k] == 1
        hi, lo = split(rm[step, k])
        parts = []
        for q in range(lanes // LANES):
            s = slice(lanes - (q + 1) * LANES, lanes - q * LANES)
            parts.append(jnp.dot(hi[:, s], flip, preferred_element_type=jnp.float32)
                         + jnp.dot(lo[:, s], flip, preferred_element_type=jnp.float32))
        return jnp.where(sampled, measured[k], r1[k] + jnp.concatenate(parts, 1))

    def gather(step, slot, d):
        own = x.at[step, slot, c, :, pl.ds(0, lanes)]
        return remote(own, own, g_send.at[step, d - 1, slot], g_recv.at[step, d - 1, slot],
                      {"coil": lax.rem(c + d, nc)})

    def outer(step):
        down = remote(x.at[step, 1, c, :, pl.ds(0, lanes)], x.at[step, planes + 1, c, :, pl.ds(0, lanes)],
                      z_send.at[step, 0], z_recv.at[step, 0], {"kz": lax.max(z - 1, 0)})
        up = remote(x.at[step, planes, c, :, pl.ds(0, lanes)], x.at[step, 0, c, :, pl.ds(0, lanes)],
                    z_send.at[step, 1], z_recv.at[step, 1], {"kz": lax.min(z + 1, nz - 1)})
        return down, up

    def side(step, slot):
        near = pl.multiple_of((1 - h) * (lanes - LANES), LANES)
        return remote(x.at[step, slot, :, :, pl.ds(near, LANES)], x.at[step, slot, :, :, pl.ds(lanes, LANES)],
                      k_send.at[step, slot], k_recv.at[step, slot], {"kx": 1 - h})

    def send(step, k):
        return remote(r2.at[step, k], rm.at[step, planes - 1 - k], m_send.at[step, k],
                      m_recv.at[step, planes - 1 - k], mirror)

    def receive(step, k):
        remote(r2.at[step, planes - 1 - k], rm.at[step, k], m_send.at[step, planes - 1 - k],
               m_recv.at[step, k], mirror).wait_recv()

    def start_outer(step):
        down, up = outer(step)

        @pl.when(z > 0)
        def _():
            down.start()

        @pl.when(z < nz - 1)
        def _():
            up.start()

    def wait_outer(step):
        down, up = outer(step)

        @pl.when(z > 0)
        def _():
            down.wait_send()
            up.wait_recv()

        @pl.when(z < nz - 1)
        def _():
            up.wait_send()
            down.wait_recv()

    def start_gather(step, n):
        for d in range(1, nc):
            gather(step, order(n, slots, step), d).start()

    def wait_gather(step, n):
        slot = order(n, slots, step)
        for d in range(1, nc):
            gather(step, slot, d).wait_recv()
        side(step, slot).start()

    def divide(step, n):
        slot = order(n, slots, step)
        side(step, slot).wait_recv()
        value = x[step, slot].reshape(nc * rows, wide)
        xh[slot], xl[slot] = split(jnp.where(keep, value, 0.0))

    def convolve(step, n):
        k = order(n, slots, step) - 1
        hi = xh[pl.ds(k, 3)].reshape(-1, wide)
        lo = xl[pl.ds(k, 3)].reshape(-1, wide)
        results = []
        for v in (1, 0):
            w = slice(v * 9 * rows, (v + 1) * 9 * rows)
            p = (jnp.dot(wh[w], hi, preferred_element_type=jnp.float32)
                 + jnp.dot(wh[w], lo, preferred_element_type=jnp.float32)
                 + jnp.dot(wl[w], hi, preferred_element_type=jnp.float32))
            total = None
            for b in (1, 0, 2):
                t = p[(3 * b + 1) * rows:(3 * b + 2) * rows]
                t = t + pltpu.roll(p[3 * b * rows:(3 * b + 1) * rows], row, 1)
                t = t + pltpu.roll(p[(3 * b + 2) * rows:(3 * b + 3) * rows], wide - row, 1)
                if b == 0:
                    t = jnp.where(after, pltpu.roll(t, 1, 1), 0.0)
                if b == 2:
                    t = jnp.where(before, pltpu.roll(t, wide - 1, 1), 0.0)
                total = t if total is None else total + t
            results.append(total[:, :lanes])
            if v:
                r2[step, k] = results[0]
        r1[k] = results[1]
        send(step, k).start()

    for step in range(ITERS):
        @pl.when(z == 0)
        def _():
            x[step, 0, c, :, :lanes] = jnp.zeros((rows, lanes), jnp.float32)

        @pl.when(z == nz - 1)
        def _():
            x[step, planes + 1, c, :, :lanes] = jnp.zeros((rows, lanes), jnp.float32)

    def first(k, _):
        x[0, k + 1, c, :, :lanes] = jnp.where(mask[k] == 1, measured[k], 0.0)
        return 0

    lax.fori_loop(0, planes, first, 0)
    start_outer(0)

    def first_gather(n, _):
        start_gather(0, n)
        return 0

    lax.fori_loop(0, planes, first_gather, 0)
    place_weights(kernel, nc, wf, wh, 0)
    wait_outer(0)
    lax.fori_loop(planes, slots, first_gather, 0)
    for n in (0, 1):
        wait_gather(0, n)
    place_weights(kernel, nc, wf, wl, 1)

    def stage(n, _):
        @pl.when(n < slots + 2)
        def _():
            divide(0, n - 2)

        @pl.when(n >= 4)
        def _():
            convolve(0, n - 4)

        @pl.when(n < slots)
        def _():
            wait_gather(0, n)

        return 0

    lax.fori_loop(2, planes + 4, stage, 0)

    for step in range(1, ITERS):
        def again(n, _):
            @pl.when(n < planes)
            def _():
                k = order(n, slots, step) - 1
                receive(step - 1, k)
                x[step, k + 1, c, :, :lanes] = combine(step - 1, k)

            @pl.when((n >= 3) & (n < planes + 3))
            def _():
                divide(step, n - 3)

            @pl.when(n == planes - 1)
            def _():
                start_outer(step)

            @pl.when(n < planes)
            def _():
                start_gather(step, n)

            @pl.when(n == planes + 1)
            def _():
                wait_outer(step)
                start_gather(step, planes)
                start_gather(step, planes + 1)

            @pl.when(n >= 5)
            def _():
                convolve(step, n - 5)

            @pl.when((n >= 2) & (n < planes + 2))
            def _():
                wait_gather(step, n - 2)

            return 0

        lax.fori_loop(0, planes + 3, again, 0)
        for n in (planes, planes + 1):
            wait_gather(step, n)

        def rest(n, _):
            divide(step, n + 2)
            convolve(step, n)
            return 0

        lax.fori_loop(planes - 2, planes, rest, 0)

    def last(n, _):
        k = order(n, slots, ITERS) - 1
        receive(ITERS - 1, k)
        out[k] = combine(ITERS - 1, k)
        return 0

    lax.fori_loop(0, planes, last, 0)

    for step in range(ITERS):
        def sent(slot, _):
            for d in range(1, nc):
                gather(step, slot, d).wait_send()
            side(step, slot).wait_send()
            return 0

        lax.fori_loop(0, slots, sent, 0)

        def mirrored(k, _):
            send(step, k).wait_send()
            return 0

        lax.fori_loop(0, planes, mirrored, 0)


def on_device(sizes, measured, mask, kernel):
    nz, nc = sizes
    _, coils, depth_x, planes, row = measured.shape
    rows, lanes = 2 * coils, depth_x * row
    wide = lanes + LANES
    flat = measured.transpose(3, 0, 1, 2, 4).reshape(planes, rows, lanes)
    sampled = mask.transpose(1, 0, 2).reshape(planes, 1, lanes)
    weights = (18 * rows, 3 * nc * rows)
    vmem = pl.BlockSpec(memory_space=pltpu.VMEM)
    dma = pltpu.SemaphoreType.DMA
    result = pl.pallas_call(
        functools.partial(body, sizes, row),
        out_shape=jax.ShapeDtypeStruct((planes, rows, lanes), jnp.float32),
        in_specs=[vmem] * 3,
        out_specs=vmem,
        scratch_shapes=[
            pltpu.VMEM((ITERS, planes + 2, nc, rows, wide), jnp.float32),
            pltpu.VMEM((planes + 2, nc * rows, wide), jnp.bfloat16),
            pltpu.VMEM((planes + 2, nc * rows, wide), jnp.bfloat16),
            pltpu.VMEM(weights, jnp.float32),
            pltpu.VMEM(weights, jnp.bfloat16),
            pltpu.VMEM(weights, jnp.bfloat16),
            pltpu.VMEM((planes, rows, lanes), jnp.float32),
            pltpu.VMEM((ITERS, planes, rows, lanes), jnp.float32),
            pltpu.VMEM((ITERS, planes, rows, lanes), jnp.float32),
            dma((ITERS, nc - 1, planes + 2)), dma((ITERS, nc - 1, planes + 2)),
            dma((ITERS, 2)), dma((ITERS, 2)),
            dma((ITERS, planes + 2)), dma((ITERS, planes + 2)),
            dma((ITERS, planes)), dma((ITERS, planes)),
        ],
        compiler_params=pltpu.CompilerParams(collective_id=0, has_side_effects=True),
    )(flat, sampled, kernel)
    result = result.reshape(planes, 2, coils, depth_x, row)
    return result.transpose(1, 2, 3, 0, 4)


def solution(mesh):
    placed = (
        P(None, ("grp", "coil"), "kx", "kz", None),
        P(("grp", "kx"), "kz", None),
        P(None, None, "coil", None),
    )
    return jax.shard_map(
        functools.partial(on_device, (mesh.shape["kz"], mesh.shape["coil"])),
        mesh=mesh,
        in_specs=placed,
        out_specs=P(None, ("grp", "coil"), "kx", "kz", None),
        check_vma=False,
    )
```
